32 devices in a mesh: mom: 8 (over z, core), bond: 4 (over y, x).
Axes of the slice: x: 2, y: 2, z: 4, core: 2. Of those that a mesh axis runs over, the one named last changes fastest.
Arguments:
- vertex: bfloat16 [3, 256, 512, 512], P(None, ('mom', 'bond')), may hold values from -6 to 6
- loop_matrix: bfloat16 [3, 256, 512, 512], P(None, ('mom', 'bond')), may hold values from -0.01171875 to 0.01171875
- own_mix: float32 [3, 3], replicated, may hold values from -4 to 4
- cross_mix: float32 [3, 3], replicated, may hold values from -4 to 4
- shells: int32 [512], replicated, may hold values from 0 to 4
- partner: int32 [512], replicated, may hold values from 0 to 511, as said below
- grid_index: int32 [256], replicated, may hold values from 0 to 255, each once
Outputs:
- flowed: bfloat16 [3, 256, 512, 512], P(None, ('mom', 'bond'))
The draws below stay inside these ranges and needn't reach their ends.
Inputs may be any that keep to these rules, and one draw needn't show every extreme that they name: partner[partner[a]] = a and partner[a] != a for every bond a; partner[a] // 64 = (a // 64 + 512 // 128) % 8. `grid_index`: each grid point appears once; point k has coordinates (k // 16, k % 16).
All inputs are finite; a program needn't handle non-finite values.
Results may differ from the reference program's by a relative error of at most 0.007.
Values may be sent and summed in bfloat16 or wider, within the bound.
A program may use at most 256 MiB of HBM per device.

```python
import math
import jax
import jax.numpy as jnp
from jax import lax

G = 16
NB = 512
NCH = 3
SHELLS = 5
Q = 256
PB = 64


def draw_partner(key, part):
    half_blocks = NB // PB // 2
    scores = jax.random.randint(key, (half_blocks, PB), 0, 1 << 20) * PB + jnp.arange(PB, dtype=jnp.int32)[None, :]
    sigma_order = jnp.argsort(scores, axis=1).astype(jnp.int32)
    inverse = jnp.argsort(sigma_order, axis=1).astype(jnp.int32)
    block_ids = jnp.arange(half_blocks, dtype=jnp.int32)[:, None]
    lower_half = (block_ids + half_blocks) * PB + sigma_order
    upper_half = block_ids * PB + inverse
    return jnp.concatenate([lower_half.reshape(-1), upper_half.reshape(-1)]).astype(jnp.int32)


def place_ends(values, key, smallest, top_value):
    extent = values.shape
    index_at = [jax.random.randint(jax.random.fold_in(key, axis), (), 0, extent[axis]) for axis in range(len(extent))]
    values = values.at[tuple(index_at)].set(smallest)
    longest = extent.index(max(extent))
    index_at[longest] = (index_at[longest] + 1) % extent[longest]
    return values.at[tuple(index_at)].set(top_value)


def block_scale(key, extent, cuts, least, top_value):
    gain, own = 1.0, jax.random.fold_in(key, 6)
    for dim, blocks in cuts:
        draws = jnp.exp(jax.random.uniform(jax.random.fold_in(own, dim), (blocks,), jnp.float32, least / len(cuts), top_value / len(cuts)))
        gain = gain * jnp.repeat(draws, extent[dim] // blocks).reshape([-1 if axis == dim else 1 for axis in range(len(extent))])
    return gain


def noise(stream_key, dims, width, limit, cuts=(), held_as=jnp.bfloat16):
    loudness = block_scale(stream_key, dims, cuts, -0.22, 0.18) if cuts else 1.0
    result = jax.random.normal(stream_key, dims, jnp.float32) * width * loudness
    return jnp.minimum(jnp.maximum(result, -limit), limit).astype(held_as)


def setup_inputs(seed: int = 0) -> dict:
    key_list = jax.random.split(jax.random.key(seed), 8)
    vertex = noise(key_list[0], (NCH, Q, NB, NB), 1.0, 6.0, ((1, 32),))
    loop_matrix = noise(key_list[1], (NCH, Q, NB, NB), (NB * NB) ** -0.5, 0.01171875, ((1, 32),))
    own_mix = noise(key_list[2], (NCH, NCH), 1.0, 4.0, (), jnp.float32)
    cross_mix = noise(key_list[3], (NCH, NCH), 1.0, 4.0, (), jnp.float32)
    shells = place_ends(jax.random.randint(key_list[4], (NB,), 0, SHELLS), jax.random.fold_in(key_list[4], 1), 0, SHELLS - 1).astype(jnp.int32)
    partner = draw_partner(jax.random.fold_in(key_list[7], 71), 0)
    grid_index = jax.random.permutation(key_list[6], Q).astype(jnp.int32)
    return {"vertex": vertex, "loop_matrix": loop_matrix, "own_mix": own_mix, "cross_mix": cross_mix, "shells": shells, "partner": partner, "grid_index": grid_index}


def cas_table(grid_index, negate):
    points = jnp.arange(Q, dtype=jnp.int32)
    disp_x = points // G
    disp_y = points % G
    wave_x = grid_index // G
    wave_y = grid_index % G
    phases = (disp_x[:, None] * wave_x[None, :] + disp_y[:, None] * wave_y[None, :]) % G
    if negate:
        phases = (G - phases) % G
    angles = phases.astype(jnp.float32) * (2.0 * math.pi / G)
    return (jnp.cos(angles) + jnp.sin(angles)).astype(jnp.bfloat16)


def cycle_index():
    points = jnp.arange(Q, dtype=jnp.int32)
    centre_x = (points // G + G // 2) % G - G // 2
    centre_y = (points % G + G // 2) % G - G // 2
    return jnp.maximum(jnp.abs(centre_x), jnp.abs(centre_y))


def reference(vertex, loop_matrix, own_mix, cross_mix, shells, partner, grid_index):
    def flow_step(operands):
        vertex_one, loop_one = operands
        vertex_wide = vertex_one.astype(jnp.float32)
        half_product = jnp.einsum("qab,qbd->qad", vertex_wide, loop_one.astype(jnp.float32)).astype(jnp.bfloat16)
        return jnp.einsum("qab,qbd->qad", half_product.astype(jnp.float32), vertex_wide)

    product = lax.map(flow_step, (vertex, loop_matrix))
    rounded = product.astype(jnp.bfloat16)
    crossed = jnp.take(jnp.take(rounded, partner, axis=2), partner, axis=3)
    plus_table = cas_table(grid_index, False).astype(jnp.float32)
    minus_table = cas_table(grid_index, True).astype(jnp.float32)
    cycle_values = cycle_index()
    height = math.gcd(NB, 64)
    block_count = NB // height
    row_width = height * NB

    def by_rows(field_data):
        return jnp.moveaxis(field_data.reshape(NCH, Q, block_count, height, NB), 2, 0)

    def lattice_step(operands):
        own_rows, cross_rows, shell_rows = operands
        own_lattice = jnp.einsum("rq,cqe->cre", plus_table, own_rows.reshape(NCH, Q, row_width).astype(jnp.float32), precision=lax.Precision.HIGHEST)
        cross_lattice = jnp.einsum("rq,cqe->cre", minus_table, cross_rows.reshape(NCH, Q, row_width).astype(jnp.float32), precision=lax.Precision.HIGHEST)
        mixed_terms = jnp.einsum("dc,cre->dre", own_mix, own_lattice, precision=lax.Precision.HIGHEST) + jnp.einsum("dc,cre->dre", cross_mix, cross_lattice, precision=lax.Precision.HIGHEST)
        reach_sum = (shell_rows[:, None] + shells[None, :]).reshape(row_width)
        kept_mask = cycle_values[:, None] <= reach_sum[None, :]
        projected = jnp.where(kept_mask[None], mixed_terms * (1.0 / Q), 0.0).astype(jnp.bfloat16)
        returned = jnp.einsum("rq,dre->dqe", plus_table, projected.astype(jnp.float32), precision=lax.Precision.HIGHEST)
        return returned.astype(jnp.bfloat16)

    pieces = lax.map(lattice_step, (by_rows(rounded), by_rows(crossed), shells.reshape(block_count, height)))
    returned = jnp.moveaxis(pieces.reshape(block_count, NCH, Q, height, NB), 0, 2).reshape(NCH, Q, NB, NB)
    flowed = vertex.astype(jnp.float32) + product + returned.astype(jnp.float32)
    return flowed.astype(jnp.bfloat16)
```

```python
import functools
import math

import jax
import jax.numpy as jnp
from jax import lax
from jax.experimental import pallas as pl
from jax.experimental.pallas import tpu as pltpu
from jax.sharding import PartitionSpec as P

LANES = 128
VMEM_LIMIT = 58 * 1024 * 1024
AXES = ("mom", "bond")


def cas_table(grid_index, negate):
    count = grid_index.shape[0]
    side = math.isqrt(count)
    points = jnp.arange(count, dtype=jnp.int32)
    disp_x = points // side
    disp_y = points % side
    wave_x = grid_index // side
    wave_y = grid_index % side
    phases = (disp_x[:, None] * wave_x[None, :] + disp_y[:, None] * wave_y[None, :]) % side
    if negate:
        phases = (side - phases) % side
    angles = phases.astype(jnp.float32) * (2.0 * math.pi / side)
    return (jnp.cos(angles) + jnp.sin(angles)).astype(jnp.bfloat16)


def cycle_index(count):
    side = math.isqrt(count)
    points = jnp.arange(count, dtype=jnp.int32)
    centre_x = (points // side + side // 2) % side - side // 2
    centre_y = (points % side + side // 2) % side - side // 2
    return jnp.maximum(jnp.abs(centre_x), jnp.abs(centre_y))


def dot(a, b):
    return jnp.dot(a, b, preferred_element_type=jnp.float32)


def product_kernel(mom_local, places, vertex_ref, loop_ref, pick_ref, spread_ref, base_ref, send_ref, wide_ref):
    step = pl.program_id(0)
    vertex = vertex_ref[0, 0]
    bonds = vertex.shape[0]
    half = bonds // 2
    group = half // places
    half_product = dot(vertex, loop_ref[0, 0]).astype(jnp.bfloat16)
    product = dot(half_product, vertex)
    base_ref[0] = (product + vertex.astype(jnp.float32)).astype(jnp.bfloat16)
    rounded = product.astype(jnp.bfloat16)
    left = rounded[:, :half]
    right = dot(rounded[:, half:], spread_ref[...]).astype(jnp.bfloat16)
    for side, part in enumerate((left, right)):
        upper = dot(pick_ref[...], part[half:])
        lower = part[:half].astype(jnp.float32)
        for lane in range(half // LANES):
            at = side * (half // LANES) + lane
            cols = slice(lane * LANES, (lane + 1) * LANES)
            if mom_local == 1:
                wide_ref[at, :half] = lower[:, cols]
                wide_ref[at, half:] = upper[:, cols]
            else:
                wide_ref[at, pl.ds(step, half, stride=mom_local), :] = lower[:, cols]
                wide_ref[at, pl.ds(half * mom_local + step, half, stride=mom_local), :] = upper[:, cols]

    @pl.when(step == mom_local - 1)
    def _():
        for at in range(bonds // LANES):
            cols = slice(at * LANES, (at + 1) * LANES)
            for side in range(2):
                piece = wide_ref[at, side * half * mom_local : (side + 1) * half * mom_local]
                send_ref[:, side, :, :, cols] = piece.reshape(places, group, mom_local, LANES).astype(jnp.bfloat16)


def lattice_kernel(channels, own_ref, cross_ref, plus_ref, minus_ref, back_ref, cycle_ref, reach_ref, *refs):
    received = refs[:channels]
    send_ref = refs[channels]
    places, _, _, mom_local, bonds = send_ref.shape
    count = places * mom_local
    half = bonds // 2
    blocks = [
        [
            received[c][:, side, 0].astype(jnp.float32).reshape(count, bonds).astype(jnp.bfloat16)
            for side in range(2)
        ]
        for c in range(channels)
    ]
    for side in range(2):
        mixed = None
        for c in range(channels):
            own = dot(plus_ref[...], blocks[c][side])
            crossed = dot(minus_ref[...], blocks[c][1 - side])
            crossed = jnp.concatenate([crossed[:, half:], crossed[:, :half]], axis=1)
            term = own_ref[c] * own + cross_ref[c] * crossed
            mixed = term if mixed is None else mixed + term
        kept = cycle_ref[...] <= reach_ref[side, 0]
        projected = jnp.where(kept, mixed, 0.0).astype(jnp.bfloat16)
        returned = dot(back_ref[...], projected)
        send_ref[:, side, 0] = returned.reshape(places, mom_local, bonds).astype(jnp.bfloat16)


def finish_kernel(mom_local, base_ref, received_ref, pick_ref, spread_ref, out_ref, wide_ref):
    step = pl.program_id(0)
    places, _, group, _, bonds = received_ref.shape
    half = bonds // 2

    @pl.when(step == 0)
    def _():
        for at in range(bonds // LANES):
            cols = slice(at * LANES, (at + 1) * LANES)
            for side in range(2):
                piece = received_ref[:, side, :, :, cols].astype(jnp.float32)
                wide_ref[at, side * half * mom_local : (side + 1) * half * mom_local] = piece.reshape(
                    half * mom_local, LANES
                )

    def rows_of(at):
        if mom_local == 1:
            return wide_ref[at]
        return wide_ref[at, pl.ds(step, bonds, stride=mom_local), :]

    tiles = half // LANES
    left = jnp.concatenate([rows_of(at) for at in range(tiles)], axis=1)
    right = jnp.concatenate([rows_of(at) for at in range(tiles, 2 * tiles)], axis=1)
    right = dot(right.astype(jnp.bfloat16), pick_ref[...])
    for side, part in enumerate((left, right)):
        cols = slice(side * half, (side + 1) * half)
        lower = part[:half]
        upper = dot(spread_ref[...], part[half:].astype(jnp.bfloat16))
        out_ref[0, :half, cols] = (base_ref[0, :half, cols].astype(jnp.float32) + lower).astype(jnp.bfloat16)
        out_ref[0, half:, cols] = (base_ref[0, half:, cols].astype(jnp.float32) + upper).astype(jnp.bfloat16)


def whole(shape):
    return pl.BlockSpec(shape, lambda i: (0,) * len(shape))


def params():
    return pltpu.CompilerParams(dimension_semantics=("arbitrary",), vmem_limit_bytes=VMEM_LIMIT)


def per_device(vertex, loop_matrix, own_mix, cross_mix, shells, partner, grid_index):
    places = lax.axis_size("mom") * lax.axis_size("bond")
    place = lax.axis_index("mom") * lax.axis_size("bond") + lax.axis_index("bond")
    channels, mom_local, bonds, _ = vertex.shape
    count = grid_index.shape[0]
    half = bonds // 2
    group = half // places
    tiles = bonds // LANES
    bf16 = jnp.bfloat16

    lower_partner = partner[:half] - half
    uppers = jnp.arange(half, dtype=jnp.int32)
    pick = (lower_partner[:, None] == uppers[None, :]).astype(bf16)
    spread = pick.T
    plus_table = cas_table(grid_index, False)
    minus_table = cas_table(grid_index, True)
    back_table = plus_table.T
    cycle = cycle_index(count)[:, None]
    shell_order = jnp.concatenate([shells[:half], jnp.take(shells, partner[:half])])
    shell_rows = lax.dynamic_slice_in_dim(shell_order.reshape(2, half), place * group, group, axis=1)
    reach = (shell_rows[:, :, None] + shell_order[None, None, :]).reshape(2, group, 1, bonds)
    own_scaled = own_mix * (1.0 / count)
    cross_scaled = cross_mix * (1.0 / count)

    flow_shape = (places, 2, group, mom_local, bonds)
    flow = jax.ShapeDtypeStruct(flow_shape, bf16)
    wide = pltpu.VMEM((tiles, bonds * mom_local, LANES), jnp.float32)
    square = (half, half)
    matmul = 2 * mom_local * bonds**3
    field_bytes = 2 * mom_local * bonds * bonds

    def exchange(field):
        return lax.all_to_all(field, AXES, split_axis=0, concat_axis=0, tiled=True)

    bases, arrived = [], []
    for c in range(channels):
        matrix = pl.BlockSpec((1, 1, bonds, bonds), lambda i, c=c: (c, i, 0, 0))
        base, outgoing = pl.pallas_call(
            functools.partial(product_kernel, mom_local, places),
            grid=(mom_local,),
            in_specs=[matrix, matrix, whole(square), whole(square)],
            out_specs=[pl.BlockSpec((1, bonds, bonds), lambda i: (i, 0, 0)), whole(flow_shape)],
            out_shape=[jax.ShapeDtypeStruct((mom_local, bonds, bonds), bf16), flow],
            scratch_shapes=[wide],
            compiler_params=params(),
            cost_estimate=pl.CostEstimate(flops=5 * matmul // 2, bytes_accessed=4 * field_bytes, transcendentals=0),
            name="product_%d" % c,
        )(vertex, loop_matrix, pick, spread)
        bases.append(base)
        arrived.append(exchange(outgoing))

    flow_block = pl.BlockSpec((places, 2, 1, mom_local, bonds), lambda i: (0, 0, i, 0, 0))
    table = whole((count, count))
    scalars = pl.BlockSpec(memory_space=pltpu.SMEM)
    finished = []
    for d in range(channels):
        outgoing = pl.pallas_call(
            functools.partial(lattice_kernel, channels),
            grid=(group,),
            in_specs=[
                scalars,
                scalars,
                table,
                table,
                table,
                whole((count, 1)),
                pl.BlockSpec((2, 1, 1, bonds), lambda i: (0, i, 0, 0)),
            ]
            + [flow_block] * channels,
            out_specs=flow_block,
            out_shape=flow,
            compiler_params=params(),
            cost_estimate=pl.CostEstimate(
                flops=(2 * channels + 1) * 2 * count * count * 2 * group * bonds,
                bytes_accessed=(channels + 1) * field_bytes,
                transcendentals=0,
            ),
            name="lattice_%d" % d,
        )(own_scaled[d], cross_scaled[d], plus_table, minus_table, back_table, cycle, reach, *arrived)
        finished.append(exchange(outgoing))

    results = []
    for d in range(channels):
        matrix = pl.BlockSpec((1, bonds, bonds), lambda i: (i, 0, 0))
        results.append(
            pl.pallas_call(
                functools.partial(finish_kernel, mom_local),
                grid=(mom_local,),
                in_specs=[matrix, whole(flow_shape), whole(square), whole(square)],
                out_specs=matrix,
                out_shape=jax.ShapeDtypeStruct((mom_local, bonds, bonds), bf16),
                scratch_shapes=[wide],
                compiler_params=params(),
                cost_estimate=pl.CostEstimate(flops=matmul // 2, bytes_accessed=3 * field_bytes, transcendentals=0),
                name="finish_%d" % d,
            )(bases[d], finished[d], pick, spread)
        )
    return jnp.stack(results)


def solution(mesh):
    in_specs = (P(None, AXES, None, None), P(None, AXES, None, None), P(), P(), P(), P(), P())
    return jax.shard_map(
        per_device, mesh=mesh, in_specs=in_specs, out_specs=P(None, AXES, None, None), check_vma=False
    )
```

```python
import functools
import math

import jax
import jax.numpy as jnp
from jax import lax
from jax.experimental import pallas as pl
from jax.experimental.pallas import tpu as pltpu
from jax.sharding import PartitionSpec as P

LANES = 128
VMEM_LIMIT = 58 * 1024 * 1024
AXES = ("mom", "bond")


def cas_table(grid_index, negate):
    count = grid_index.shape[0]
    side = math.isqrt(count)
    points = jnp.arange(count, dtype=jnp.int32)
    disp_x = points // side
    disp_y = points % side
    wave_x = grid_index // side
    wave_y = grid_index % side
    phases = (disp_x[:, None] * wave_x[None, :] + disp_y[:, None] * wave_y[None, :]) % side
    if negate:
        phases = (side - phases) % side
    angles = phases.astype(jnp.float32) * (2.0 * math.pi / side)
    return (jnp.cos(angles) + jnp.sin(angles)).astype(jnp.bfloat16)


def cycle_index(count):
    side = math.isqrt(count)
    points = jnp.arange(count, dtype=jnp.int32)
    centre_x = (points // side + side // 2) % side - side // 2
    centre_y = (points % side + side // 2) % side - side // 2
    return jnp.maximum(jnp.abs(centre_x), jnp.abs(centre_y))


def dot(a, b):
    return jnp.dot(a, b, preferred_element_type=jnp.float32)


def product_kernel(mom_local, places, vertex_ref, loop_ref, pick_ref, spread_ref, *refs):
    base_ref, send_ref, token_ref, wide_ref = refs[-4:]
    step = pl.program_id(1)
    token_ref[...] = jnp.zeros_like(token_ref)
    vertex = vertex_ref[0, 0]
    bonds = vertex.shape[0]
    half = bonds // 2
    group = half // places
    half_product = dot(vertex, loop_ref[0, 0]).astype(jnp.bfloat16)
    product = dot(half_product, vertex)
    base_ref[0, 0] = (product + vertex.astype(jnp.float32)).astype(jnp.bfloat16)
    rounded = product.astype(jnp.bfloat16)
    left = rounded[:, :half]
    right = dot(rounded[:, half:], spread_ref[...]).astype(jnp.bfloat16)
    for side, part in enumerate((left, right)):
        upper = dot(pick_ref[...], part[half:])
        lower = part[:half].astype(jnp.float32)
        for lane in range(half // LANES):
            at = side * (half // LANES) + lane
            cols = slice(lane * LANES, (lane + 1) * LANES)
            if mom_local == 1:
                wide_ref[at, :half] = lower[:, cols]
                wide_ref[at, half:] = upper[:, cols]
            else:
                wide_ref[at, pl.ds(step, half, stride=mom_local), :] = lower[:, cols]
                wide_ref[at, pl.ds(half * mom_local + step, half, stride=mom_local), :] = upper[:, cols]

    @pl.when(step == mom_local - 1)
    def _():
        for at in range(bonds // LANES):
            cols = slice(at * LANES, (at + 1) * LANES)
            for side in range(2):
                piece = wide_ref[at, side * half * mom_local : (side + 1) * half * mom_local]
                send_ref[:, 0, side, :, :, cols] = piece.reshape(places, group, mom_local, LANES).astype(jnp.bfloat16)


def lattice_kernel(sizes, targets, own_ref, cross_ref, plus_ref, minus_ref, back_ref, cycle_ref, reach_ref, *refs):
    received = [(refs[k], n) for k, size in enumerate(sizes) for n in range(size)]
    send_ref = refs[-1]
    places, _, _, _, mom_local, bonds = send_ref.shape
    count = places * mom_local
    half = bonds // 2
    blocks = [
        [
            ref[:, n, side, 0].astype(jnp.float32).reshape(count, bonds).astype(jnp.bfloat16)
            for side in range(2)
        ]
        for ref, n in received
    ]
    for side in range(2):
        mixed = [None] * len(targets)
        for c in range(len(received)):
            own = dot(plus_ref[...], blocks[c][side])
            crossed = dot(minus_ref[...], blocks[c][1 - side])
            crossed = jnp.concatenate([crossed[:, half:], crossed[:, :half]], axis=1)
            for k, d in enumerate(targets):
                term = own_ref[d, c] * own + cross_ref[d, c] * crossed
                mixed[k] = term if c == 0 else mixed[k] + term
        kept = cycle_ref[...] <= reach_ref[side, 0]
        for k in range(len(targets)):
            projected = jnp.where(kept, mixed[k], 0.0).astype(jnp.bfloat16)
            returned = dot(back_ref[...], projected)
            send_ref[:, k, side, 0] = returned.reshape(places, mom_local, bonds).astype(jnp.bfloat16)


def finish_kernel(mom_local, base_ref, received_ref, pick_ref, spread_ref, out_ref, wide_ref):
    step = pl.program_id(1)
    places, _, _, group, _, bonds = received_ref.shape
    half = bonds // 2

    @pl.when(step == 0)
    def _():
        for at in range(bonds // LANES):
            cols = slice(at * LANES, (at + 1) * LANES)
            for side in range(2):
                piece = received_ref[:, 0, side, :, :, cols].astype(jnp.float32)
                wide_ref[at, side * half * mom_local : (side + 1) * half * mom_local] = piece.reshape(
                    half * mom_local, LANES
                )

    def rows_of(at):
        if mom_local == 1:
            return wide_ref[at]
        return wide_ref[at, pl.ds(step, bonds, stride=mom_local), :]

    tiles = half // LANES
    left = jnp.concatenate([rows_of(at) for at in range(tiles)], axis=1)
    right = jnp.concatenate([rows_of(at) for at in range(tiles, 2 * tiles)], axis=1)
    right = dot(right.astype(jnp.bfloat16), pick_ref[...])
    for side, part in enumerate((left, right)):
        cols = slice(side * half, (side + 1) * half)
        lower = part[:half]
        upper = dot(spread_ref[...], part[half:].astype(jnp.bfloat16))
        out_ref[0, 0, :half, cols] = (base_ref[0, 0, :half, cols].astype(jnp.float32) + lower).astype(jnp.bfloat16)
        out_ref[0, 0, half:, cols] = (base_ref[0, 0, half:, cols].astype(jnp.float32) + upper).astype(jnp.bfloat16)


def whole(shape):
    return pl.BlockSpec(shape, lambda *steps: (0,) * len(shape))


def params(axes):
    return pltpu.CompilerParams(dimension_semantics=("arbitrary",) * axes, vmem_limit_bytes=VMEM_LIMIT)


def per_device(vertex, loop_matrix, own_mix, cross_mix, shells, partner, grid_index):
    places = lax.axis_size("mom") * lax.axis_size("bond")
    place = lax.axis_index("mom") * lax.axis_size("bond") + lax.axis_index("bond")
    channels, mom_local, bonds, _ = vertex.shape
    count = grid_index.shape[0]
    half = bonds // 2
    group = half // places
    tiles = bonds // LANES
    bf16 = jnp.bfloat16
    first = list(range(channels))
    send_groups = [first[:1], first[1:]]
    back_groups = [first[:-1], first[-1:]]

    lower_partner = partner[:half] - half
    uppers = jnp.arange(half, dtype=jnp.int32)
    pick = (lower_partner[:, None] == uppers[None, :]).astype(bf16)
    spread = pick.T

    wide = pltpu.VMEM((tiles, bonds * mom_local, LANES), jnp.float32)
    square = (half, half)
    matmul = 2 * mom_local * bonds**3
    field_bytes = 2 * mom_local * bonds * bonds
    field = jax.ShapeDtypeStruct(vertex.shape, bf16)
    token_shape = jax.ShapeDtypeStruct((8, LANES), jnp.float32)

    def flow(members):
        return jax.ShapeDtypeStruct((places, members, 2, group, mom_local, bonds), bf16)

    def one_flow():
        return pl.BlockSpec((places, 1, 2, group, mom_local, bonds), lambda c, i: (0, c, 0, 0, 0, 0))

    def matrix_at(start):
        return pl.BlockSpec((1, 1, bonds, bonds), lambda c, i: (c + start, i, 0, 0))

    def exchange(outgoing):
        return lax.all_to_all(outgoing, AXES, split_axis=0, concat_axis=0, tiled=True)

    base, token, arrived = None, None, []
    for members in send_groups:
        matrix = matrix_at(members[0])
        size = len(members)
        carried = [] if base is None else [base]
        base, outgoing, made = pl.pallas_call(
            functools.partial(product_kernel, mom_local, places),
            grid=(size, mom_local),
            in_specs=[matrix, matrix, whole(square), whole(square)]
            + [pl.BlockSpec(memory_space=pl.ANY)] * len(carried),
            out_specs=[matrix, one_flow(), whole(token_shape.shape)],
            out_shape=[field, flow(size), token_shape],
            input_output_aliases={4: 0} if carried else {},
            scratch_shapes=[wide],
            compiler_params=params(2),
            cost_estimate=pl.CostEstimate(
                flops=5 * size * matmul // 2, bytes_accessed=4 * size * field_bytes, transcendentals=0
            ),
            name="product_%d" % members[0],
        )(vertex, loop_matrix, pick, spread, *carried)
        token = made if token is None else token
        arrived.append(exchange(outgoing))

    shells, partner, grid_index, own_mix, cross_mix, _ = lax.optimization_barrier(
        (shells, partner, grid_index, own_mix, cross_mix, token)
    )
    plus_table = cas_table(grid_index, False)
    minus_table = cas_table(grid_index, True)
    back_table = plus_table.T
    cycle = cycle_index(count)[:, None]
    shell_order = jnp.concatenate([shells[:half], jnp.take(shells, partner[:half])])
    shell_rows = lax.dynamic_slice_in_dim(shell_order.reshape(2, half), place * group, group, axis=1)
    reach = (shell_rows[:, :, None] + shell_order[None, None, :]).reshape(2, group, 1, bonds)
    own_scaled = own_mix * (1.0 / count)
    cross_scaled = cross_mix * (1.0 / count)

    def row_block(members):
        return pl.BlockSpec((places, members, 2, 1, mom_local, bonds), lambda i: (0, 0, 0, i, 0, 0))

    table = whole((count, count))
    scalars = pl.BlockSpec(memory_space=pltpu.SMEM)
    sizes = [len(members) for members in send_groups]
    finished, earlier = [], []
    for members in back_groups:
        size = len(members)
        outgoing = pl.pallas_call(
            functools.partial(lattice_kernel, sizes, members),
            grid=(group,),
            in_specs=[
                scalars,
                scalars,
                table,
                table,
                table,
                whole((count, 1)),
                pl.BlockSpec((2, 1, 1, bonds), lambda i: (0, i, 0, 0)),
            ]
            + [row_block(n) for n in sizes]
            + [pl.BlockSpec(memory_space=pl.ANY)] * len(earlier),
            out_specs=row_block(size),
            out_shape=flow(size),
            compiler_params=params(1),
            cost_estimate=pl.CostEstimate(
                flops=(2 * channels + size) * 2 * count * count * 2 * group * bonds,
                bytes_accessed=(channels + size) * field_bytes,
                transcendentals=0,
            ),
            name="lattice_%d" % members[0],
        )(own_scaled, cross_scaled, plus_table, minus_table, back_table, cycle, reach, *arrived, *earlier)
        earlier = [outgoing]
        finished.append(exchange(outgoing))

    for members, received in zip(back_groups, finished):
        matrix = matrix_at(members[0])
        size = len(members)
        base = pl.pallas_call(
            functools.partial(finish_kernel, mom_local),
            grid=(size, mom_local),
            in_specs=[matrix, one_flow(), whole(square), whole(square)],
            out_specs=matrix,
            out_shape=field,
            input_output_aliases={0: 0},
            scratch_shapes=[wide],
            compiler_params=params(2),
            cost_estimate=pl.CostEstimate(
                flops=size * matmul // 2, bytes_accessed=3 * size * field_bytes, transcendentals=0
            ),
            name="finish_%d" % members[0],
        )(base, received, pick, spread)
    return base


def solution(mesh):
    in_specs = (P(None, AXES, None, None), P(None, AXES, None, None), P(), P(), P(), P(), P())
    return jax.shard_map(
        per_device, mesh=mesh, in_specs=in_specs, out_specs=P(None, AXES, None, None), check_vma=False
    )
```

```python
import functools
import math

import jax
import jax.numpy as jnp
from jax import lax
from jax.experimental import pallas as pl
from jax.experimental.layout import Layout, with_layout_constraint
from jax.experimental.pallas import tpu as pltpu
from jax.sharding import PartitionSpec as P

LANES = 128
PAIR = 2
VMEM_LIMIT = 58 * 1024 * 1024
AXES = ("mom", "bond")


def cas_table(grid_index, negate):
    count = grid_index.shape[0]
    side = math.isqrt(count)
    points = jnp.arange(count, dtype=jnp.int32)
    disp_x = points // side
    disp_y = points % side
    wave_x = grid_index // side
    wave_y = grid_index % side
    phases = (disp_x[:, None] * wave_x[None, :] + disp_y[:, None] * wave_y[None, :]) % side
    if negate:
        phases = (side - phases) % side
    angles = phases.astype(jnp.float32) * (2.0 * math.pi / side)
    return (jnp.cos(angles) + jnp.sin(angles)).astype(jnp.bfloat16)


def cycle_index(count):
    side = math.isqrt(count)
    points = jnp.arange(count, dtype=jnp.int32)
    centre_x = (points // side + side // 2) % side - side // 2
    centre_y = (points % side + side // 2) % side - side // 2
    return jnp.maximum(jnp.abs(centre_x), jnp.abs(centre_y))


def dot(a, b):
    return jnp.dot(a, b, preferred_element_type=jnp.float32)


def product_kernel(mom_local, places, vertex_ref, loop_ref, pick_ref, spread_ref, *refs):
    base_ref, send_ref, token_ref, wide_ref = refs[-4:]
    step = pl.program_id(1)
    token_ref[...] = jnp.zeros_like(token_ref)
    vertex = vertex_ref[0, 0]
    bonds = vertex.shape[0]
    half = bonds // 2
    group = half // places
    half_product = dot(vertex, loop_ref[0, 0]).astype(jnp.bfloat16)
    product = dot(half_product, vertex)
    base_ref[0, 0] = (product + vertex.astype(jnp.float32)).astype(jnp.bfloat16)
    rounded = product.astype(jnp.bfloat16)
    left = rounded[:, :half]
    right = dot(rounded[:, half:], spread_ref[...]).astype(jnp.bfloat16)
    for side, part in enumerate((left, right)):
        upper = dot(pick_ref[...], part[half:])
        lower = part[:half].astype(jnp.float32)
        for lane in range(half // LANES):
            at = side * (half // LANES) + lane
            cols = slice(lane * LANES, (lane + 1) * LANES)
            if mom_local == 1:
                wide_ref[at, :half] = lower[:, cols]
                wide_ref[at, half:] = upper[:, cols]
            else:
                wide_ref[at, pl.ds(step, half, stride=mom_local), :] = lower[:, cols]
                wide_ref[at, pl.ds(half * mom_local + step, half, stride=mom_local), :] = upper[:, cols]

    @pl.when(step == mom_local - 1)
    def _():
        for at in range(bonds // LANES):
            cols = slice(at * LANES, (at + 1) * LANES)
            for side in range(2):
                piece = wide_ref[at, side * half * mom_local : (side + 1) * half * mom_local]
                send_ref[:, 0, side, :, :, cols] = piece.reshape(places, group, mom_local, LANES).astype(jnp.bfloat16)


def first_product_kernel(places, vertex_ref, loop_ref, pick_ref, spread_ref, base_ref, send_ref, token_ref):
    token_ref[...] = jnp.zeros_like(token_ref)
    bonds = vertex_ref.shape[-1]
    half = bonds // 2
    group = half // places
    for n in range(vertex_ref.shape[1]):
        vertex = vertex_ref[0, n]
        half_product = dot(vertex, loop_ref[0, n]).astype(jnp.bfloat16)
        product = dot(half_product, vertex)
        base_ref[0, n] = (product + vertex.astype(jnp.float32)).astype(jnp.bfloat16)
        rounded = product.astype(jnp.bfloat16)
        left = rounded[:, :half]
        right = dot(rounded[:, half:], spread_ref[...]).astype(jnp.bfloat16)
        for side, part in enumerate((left, right)):
            cols = slice(side * half, (side + 1) * half)
            lower = part[:half].astype(jnp.float32)
            upper = dot(pick_ref[...], part[half:])
            send_ref[:, 0, n, 0, :, cols] = lower.reshape(places, group, half).astype(jnp.bfloat16)
            send_ref[:, 0, n, 1, :, cols] = upper.reshape(places, group, half).astype(jnp.bfloat16)


def lattice_kernel(sizes, targets, own_ref, cross_ref, plus_ref, minus_ref, back_ref, cycle_ref, reach_ref, *refs):
    received = [(refs[k], n) for k, size in enumerate(sizes) for n in range(size)]
    send_ref = refs[-1]
    places, _, _, _, mom_local, bonds = send_ref.shape
    count = places * mom_local
    half = bonds // 2
    blocks = [
        [
            ref[:, n, side, 0].astype(jnp.float32).reshape(count, bonds).astype(jnp.bfloat16)
            for side in range(2)
        ]
        for ref, n in received
    ]
    for side in range(2):
        mixed = [None] * len(targets)
        for c in range(len(received)):
            own = dot(plus_ref[...], blocks[c][side])
            crossed = dot(minus_ref[...], blocks[c][1 - side])
            crossed = jnp.concatenate([crossed[:, half:], crossed[:, :half]], axis=1)
            for k, d in enumerate(targets):
                term = own_ref[d, c] * own + cross_ref[d, c] * crossed
                mixed[k] = term if c == 0 else mixed[k] + term
        kept = cycle_ref[...] <= reach_ref[side, 0]
        for k in range(len(targets)):
            projected = jnp.where(kept, mixed[k], 0.0).astype(jnp.bfloat16)
            returned = dot(back_ref[...], projected)
            send_ref[:, k, side, 0] = returned.reshape(places, mom_local, bonds).astype(jnp.bfloat16)


def finish_kernel(mom_local, base_ref, received_ref, pick_ref, spread_ref, out_ref, wide_ref):
    step = pl.program_id(1)
    places, _, _, group, _, bonds = received_ref.shape
    half = bonds // 2

    @pl.when(step == 0)
    def _():
        for at in range(bonds // LANES):
            cols = slice(at * LANES, (at + 1) * LANES)
            for side in range(2):
                piece = received_ref[:, 0, side, :, :, cols].astype(jnp.float32)
                wide_ref[at, side * half * mom_local : (side + 1) * half * mom_local] = piece.reshape(
                    half * mom_local, LANES
                )

    def rows_of(at):
        if mom_local == 1:
            return wide_ref[at]
        return wide_ref[at, pl.ds(step, bonds, stride=mom_local), :]

    tiles = half // LANES
    left = jnp.concatenate([rows_of(at) for at in range(tiles)], axis=1)
    right = jnp.concatenate([rows_of(at) for at in range(tiles, 2 * tiles)], axis=1)
    right = dot(right.astype(jnp.bfloat16), pick_ref[...])
    for side, part in enumerate((left, right)):
        cols = slice(side * half, (side + 1) * half)
        lower = part[:half]
        upper = dot(spread_ref[...], part[half:].astype(jnp.bfloat16))
        out_ref[0, 0, :half, cols] = (base_ref[0, 0, :half, cols].astype(jnp.float32) + lower).astype(jnp.bfloat16)
        out_ref[0, 0, half:, cols] = (base_ref[0, 0, half:, cols].astype(jnp.float32) + upper).astype(jnp.bfloat16)


def last_finish_kernel(base_ref, received_ref, pick_ref, spread_ref, out_ref):
    bonds = base_ref.shape[-1]
    half = bonds // 2
    for n in range(base_ref.shape[1]):
        for side in range(2):
            cols = slice(side * half, (side + 1) * half)
            lower = received_ref[:, 0, n, 0, :, cols].astype(jnp.float32).reshape(half, half)
            upper = received_ref[:, 0, n, 1, :, cols].astype(jnp.float32).reshape(half, half).astype(jnp.bfloat16)
            if side:
                lower = dot(lower.astype(jnp.bfloat16), pick_ref[...])
                upper = dot(upper, pick_ref[...]).astype(jnp.bfloat16)
            upper = dot(spread_ref[...], upper)
            out_ref[0, n, :half, cols] = (base_ref[0, n, :half, cols].astype(jnp.float32) + lower).astype(jnp.bfloat16)
            out_ref[0, n, half:, cols] = (base_ref[0, n, half:, cols].astype(jnp.float32) + upper).astype(jnp.bfloat16)


def whole(shape):
    return pl.BlockSpec(shape, lambda *steps: (0,) * len(shape))


def params(axes):
    return pltpu.CompilerParams(dimension_semantics=("arbitrary",) * axes, vmem_limit_bytes=VMEM_LIMIT)


def per_device(vertex, loop_matrix, own_mix, cross_mix, shells, partner, grid_index):
    places = lax.axis_size("mom") * lax.axis_size("bond")
    place = lax.axis_index("mom") * lax.axis_size("bond") + lax.axis_index("bond")
    channels, mom_local, bonds, _ = vertex.shape
    count = grid_index.shape[0]
    half = bonds // 2
    group = half // places
    tiles = bonds // LANES
    bf16 = jnp.bfloat16
    first = list(range(channels))
    send_groups = [first[:1], first[1:]]
    back_groups = [first[:-1], first[-1:]]

    lower_partner = partner[:half] - half
    uppers = jnp.arange(half, dtype=jnp.int32)
    pick = (lower_partner[:, None] == uppers[None, :]).astype(bf16)
    spread = pick.T

    wide = pltpu.VMEM((tiles, bonds * mom_local, LANES), jnp.float32)
    square = (half, half)
    matmul = 2 * mom_local * bonds**3
    field_bytes = 2 * mom_local * bonds * bonds
    field = jax.ShapeDtypeStruct(vertex.shape, bf16)
    token_shape = jax.ShapeDtypeStruct((8, LANES), jnp.float32)

    def flow(members):
        return jax.ShapeDtypeStruct((places, members, 2, group, mom_local, bonds), bf16)

    def one_flow():
        return pl.BlockSpec((places, 1, 2, group, mom_local, bonds), lambda c, i: (0, c, 0, 0, 0, 0))

    def matrix_at(start):
        return pl.BlockSpec((1, 1, bonds, bonds), lambda c, i: (c + start, i, 0, 0))

    def exchange(outgoing):
        return lax.all_to_all(outgoing, AXES, split_axis=0, concat_axis=0, tiled=True)

    pair = PAIR if mom_local % PAIR == 0 else 1
    plain = jax.ShapeDtypeStruct((places, 1, mom_local, 2, group, bonds), bf16)
    plain_block = pl.BlockSpec((places, 1, pair, 2, group, bonds), lambda i: (0, 0, i, 0, 0, 0))

    def pair_at(start):
        return pl.BlockSpec((1, pair, bonds, bonds), lambda i: (start, i, 0, 0))

    base, outgoing, token = pl.pallas_call(
        functools.partial(first_product_kernel, places),
        grid=(mom_local // pair,),
        in_specs=[pair_at(0), pair_at(0), whole(square), whole(square)],
        out_specs=[pair_at(0), plain_block, whole(token_shape.shape)],
        out_shape=[field, plain, token_shape],
        compiler_params=params(1),
        cost_estimate=pl.CostEstimate(flops=5 * matmul // 2, bytes_accessed=4 * field_bytes, transcendentals=0),
        name="product_first",
    )(vertex, loop_matrix, pick, spread)
    whole_rows = with_layout_constraint(exchange(outgoing), Layout(major_to_minor=tuple(range(6))))
    arrived = [whole_rows.transpose(0, 1, 3, 4, 2, 5)]
    for members in send_groups[1:]:
        matrix = matrix_at(members[0])
        size = len(members)
        base, outgoing, _ = pl.pallas_call(
            functools.partial(product_kernel, mom_local, places),
            grid=(size, mom_local),
            in_specs=[matrix, matrix, whole(square), whole(square)]
            + [pl.BlockSpec(memory_space=pl.ANY)],
            out_specs=[matrix, one_flow(), whole(token_shape.shape)],
            out_shape=[field, flow(size), token_shape],
            input_output_aliases={4: 0},
            scratch_shapes=[wide],
            compiler_params=params(2),
            cost_estimate=pl.CostEstimate(
                flops=5 * size * matmul // 2, bytes_accessed=4 * size * field_bytes, transcendentals=0
            ),
            name="product_%d" % members[0],
        )(vertex, loop_matrix, pick, spread, base)
        arrived.append(exchange(outgoing))

    shells, partner, grid_index, own_mix, cross_mix, _ = lax.optimization_barrier(
        (shells, partner, grid_index, own_mix, cross_mix, token)
    )
    plus_table = cas_table(grid_index, False)
    minus_table = cas_table(grid_index, True)
    back_table = plus_table.T
    cycle = cycle_index(count)[:, None]
    shell_order = jnp.concatenate([shells[:half], jnp.take(shells, partner[:half])])
    shell_rows = lax.dynamic_slice_in_dim(shell_order.reshape(2, half), place * group, group, axis=1)
    reach = (shell_rows[:, :, None] + shell_order[None, None, :]).reshape(2, group, 1, bonds)
    own_scaled = own_mix * (1.0 / count)
    cross_scaled = cross_mix * (1.0 / count)

    def row_block(members):
        return pl.BlockSpec((places, members, 2, 1, mom_local, bonds), lambda i: (0, 0, 0, i, 0, 0))

    table = whole((count, count))
    scalars = pl.BlockSpec(memory_space=pltpu.SMEM)
    sizes = [len(members) for members in send_groups]
    finished, earlier = [], []
    for members in back_groups:
        size = len(members)
        outgoing = pl.pallas_call(
            functools.partial(lattice_kernel, sizes, members),
            grid=(group,),
            in_specs=[
                scalars,
                scalars,
                table,
                table,
                table,
                whole((count, 1)),
                pl.BlockSpec((2, 1, 1, bonds), lambda i: (0, i, 0, 0)),
            ]
            + [row_block(n) for n in sizes]
            + [pl.BlockSpec(memory_space=pl.ANY)] * len(earlier),
            out_specs=row_block(size),
            out_shape=flow(size),
            compiler_params=params(1),
            cost_estimate=pl.CostEstimate(
                flops=(2 * channels + size) * 2 * count * count * 2 * group * bonds,
                bytes_accessed=(channels + size) * field_bytes,
                transcendentals=0,
            ),
            name="lattice_%d" % members[0],
        )(own_scaled, cross_scaled, plus_table, minus_table, back_table, cycle, reach, *arrived, *earlier)
        earlier = [outgoing]
        if members is back_groups[-1]:
            outgoing = outgoing.transpose(0, 1, 4, 2, 3, 5)
        finished.append(exchange(outgoing))

    for members, received in zip(back_groups[:-1], finished[:-1]):
        matrix = matrix_at(members[0])
        size = len(members)
        base = pl.pallas_call(
            functools.partial(finish_kernel, mom_local),
            grid=(size, mom_local),
            in_specs=[matrix, one_flow(), whole(square), whole(square)],
            out_specs=matrix,
            out_shape=field,
            input_output_aliases={0: 0},
            scratch_shapes=[wide],
            compiler_params=params(2),
            cost_estimate=pl.CostEstimate(
                flops=size * matmul // 2, bytes_accessed=3 * size * field_bytes, transcendentals=0
            ),
            name="finish_%d" % members[0],
        )(base, received, pick, spread)
    last = back_groups[-1][0]
    return pl.pallas_call(
        last_finish_kernel,
        grid=(mom_local // pair,),
        in_specs=[pair_at(last), plain_block, whole(square), whole(square)],
        out_specs=pair_at(last),
        out_shape=field,
        input_output_aliases={0: 0},
        compiler_params=params(1),
        cost_estimate=pl.CostEstimate(flops=matmul // 2, bytes_accessed=3 * field_bytes, transcendentals=0),
        name="finish_last",
    )(base, finished[-1], pick, spread)


def solution(mesh):
    in_specs = (P(None, AXES, None, None), P(None, AXES, None, None), P(), P(), P(), P(), P())
    return jax.shard_map(
        per_device, mesh=mesh, in_specs=in_specs, out_specs=P(None, AXES, None, None), check_vma=False
    )
```

```python
import functools
import math

import jax
import jax.numpy as jnp
from jax import lax
from jax.experimental import pallas as pl
from jax.experimental.layout import Layout, with_layout_constraint
from jax.experimental.pallas import tpu as pltpu
from jax.sharding import PartitionSpec as P

LANES = 128
PAIR = 2
ROWS = 2
VMEM_LIMIT = 58 * 1024 * 1024
AXES = ("mom", "bond")


def cas_table(grid_index, negate):
    count = grid_index.shape[0]
    side = math.isqrt(count)
    points = jnp.arange(count, dtype=jnp.int32)
    disp_x = points // side
    disp_y = points % side
    wave_x = grid_index // side
    wave_y = grid_index % side
    phases = (disp_x[:, None] * wave_x[None, :] + disp_y[:, None] * wave_y[None, :]) % side
    if negate:
        phases = (side - phases) % side
    angles = phases.astype(jnp.float32) * (2.0 * math.pi / side)
    return (jnp.cos(angles) + jnp.sin(angles)).astype(jnp.bfloat16)


def cycle_index(count):
    side = math.isqrt(count)
    points = jnp.arange(count, dtype=jnp.int32)
    centre_x = (points // side + side // 2) % side - side // 2
    centre_y = (points % side + side // 2) % side - side // 2
    return jnp.maximum(jnp.abs(centre_x), jnp.abs(centre_y))


def dot(a, b):
    return jnp.dot(a, b, preferred_element_type=jnp.float32)


def product_kernel(mom_local, places, vertex_ref, loop_ref, pick_ref, spread_ref, *refs):
    base_ref, send_ref, token_ref, wide_ref = refs[-4:]
    step = pl.program_id(1)
    token_ref[...] = jnp.zeros_like(token_ref)
    vertex = vertex_ref[0, 0]
    bonds = vertex.shape[0]
    half = bonds // 2
    group = half // places
    half_product = dot(vertex, loop_ref[0, 0]).astype(jnp.bfloat16)
    product = dot(half_product, vertex)
    base_ref[0, 0] = (product + vertex.astype(jnp.float32)).astype(jnp.bfloat16)
    rounded = product.astype(jnp.bfloat16)
    left = rounded[:, :half]
    right = dot(rounded[:, half:], spread_ref[...]).astype(jnp.bfloat16)
    for side, part in enumerate((left, right)):
        upper = dot(pick_ref[...], part[half:])
        lower = part[:half].astype(jnp.float32)
        for lane in range(half // LANES):
            at = side * (half // LANES) + lane
            cols = slice(lane * LANES, (lane + 1) * LANES)
            if mom_local == 1:
                wide_ref[at, :half] = lower[:, cols]
                wide_ref[at, half:] = upper[:, cols]
            else:
                wide_ref[at, pl.ds(step, half, stride=mom_local), :] = lower[:, cols]
                wide_ref[at, pl.ds(half * mom_local + step, half, stride=mom_local), :] = upper[:, cols]

    @pl.when(step == mom_local - 1)
    def _():
        for at in range(bonds // LANES):
            cols = slice(at * LANES, (at + 1) * LANES)
            for side in range(2):
                piece = wide_ref[at, side * half * mom_local : (side + 1) * half * mom_local]
                send_ref[:, 0, side, :, :, cols] = piece.reshape(places, group, mom_local, LANES).astype(jnp.bfloat16)


def first_product_kernel(places, vertex_ref, loop_ref, pick_ref, spread_ref, base_ref, send_ref, token_ref):
    token_ref[...] = jnp.zeros_like(token_ref)
    bonds = vertex_ref.shape[-1]
    half = bonds // 2
    group = half // places
    for n in range(vertex_ref.shape[1]):
        vertex = vertex_ref[0, n]
        half_product = dot(vertex, loop_ref[0, n]).astype(jnp.bfloat16)
        product = dot(half_product, vertex)
        base_ref[0, n] = (product + vertex.astype(jnp.float32)).astype(jnp.bfloat16)
        rounded = product.astype(jnp.bfloat16)
        left = rounded[:, :half]
        right = dot(rounded[:, half:], spread_ref[...]).astype(jnp.bfloat16)
        for side, part in enumerate((left, right)):
            cols = slice(side * half, (side + 1) * half)
            lower = part[:half].astype(jnp.float32)
            upper = dot(pick_ref[...], part[half:])
            send_ref[:, 0, n, 0, :, cols] = lower.reshape(places, group, half).astype(jnp.bfloat16)
            send_ref[:, 0, n, 1, :, cols] = upper.reshape(places, group, half).astype(jnp.bfloat16)


def lattice_kernel(sizes, targets, own_ref, cross_ref, plus_ref, minus_ref, back_ref, cycle_ref, reach_ref, *refs):
    received = [(refs[k], n) for k, size in enumerate(sizes) for n in range(size)]
    send_ref = refs[-1]
    places, _, _, _, mom_local, bonds = send_ref.shape
    count = places * mom_local
    half = bonds // 2
    for row in range(send_ref.shape[3]):
        blocks = [
            [
                ref[:, n, side, row].astype(jnp.float32).reshape(count, bonds).astype(jnp.bfloat16)
                for side in range(2)
            ]
            for ref, n in received
        ]
        for side in range(2):
            mixed = [None] * len(targets)
            for c in range(len(received)):
                own = dot(plus_ref[...], blocks[c][side])
                crossed = dot(minus_ref[...], blocks[c][1 - side])
                crossed = jnp.concatenate([crossed[:, half:], crossed[:, :half]], axis=1)
                for k, d in enumerate(targets):
                    term = own_ref[d, c] * own + cross_ref[d, c] * crossed
                    mixed[k] = term if c == 0 else mixed[k] + term
            kept = cycle_ref[...] <= reach_ref[side, row]
            for k in range(len(targets)):
                projected = jnp.where(kept, mixed[k], 0.0).astype(jnp.bfloat16)
                returned = dot(back_ref[...], projected)
                send_ref[:, k, side, row] = returned.reshape(places, mom_local, bonds).astype(jnp.bfloat16)


def finish_kernel(mom_local, base_ref, received_ref, pick_ref, spread_ref, out_ref, wide_ref):
    step = pl.program_id(1)
    places, _, _, group, _, bonds = received_ref.shape
    half = bonds // 2

    @pl.when(step == 0)
    def _():
        for at in range(bonds // LANES):
            cols = slice(at * LANES, (at + 1) * LANES)
            for side in range(2):
                piece = received_ref[:, 0, side, :, :, cols].astype(jnp.float32)
                wide_ref[at, side * half * mom_local : (side + 1) * half * mom_local] = piece.reshape(
                    half * mom_local, LANES
                )

    def rows_of(at):
        if mom_local == 1:
            return wide_ref[at]
        return wide_ref[at, pl.ds(step, bonds, stride=mom_local), :]

    tiles = half // LANES
    left = jnp.concatenate([rows_of(at) for at in range(tiles)], axis=1)
    right = jnp.concatenate([rows_of(at) for at in range(tiles, 2 * tiles)], axis=1)
    right = dot(right.astype(jnp.bfloat16), pick_ref[...])
    for side, part in enumerate((left, right)):
        cols = slice(side * half, (side + 1) * half)
        lower = part[:half]
        upper = dot(spread_ref[...], part[half:].astype(jnp.bfloat16))
        out_ref[0, 0, :half, cols] = (base_ref[0, 0, :half, cols].astype(jnp.float32) + lower).astype(jnp.bfloat16)
        out_ref[0, 0, half:, cols] = (base_ref[0, 0, half:, cols].astype(jnp.float32) + upper).astype(jnp.bfloat16)


def last_finish_kernel(base_ref, received_ref, pick_ref, spread_ref, out_ref):
    bonds = base_ref.shape[-1]
    half = bonds // 2
    for n in range(base_ref.shape[1]):
        for side in range(2):
            cols = slice(side * half, (side + 1) * half)
            lower = received_ref[:, 0, n, 0, :, cols].astype(jnp.float32).reshape(half, half)
            upper = received_ref[:, 0, n, 1, :, cols].astype(jnp.float32).reshape(half, half).astype(jnp.bfloat16)
            if side:
                lower = dot(lower.astype(jnp.bfloat16), pick_ref[...])
                upper = dot(upper, pick_ref[...]).astype(jnp.bfloat16)
            upper = dot(spread_ref[...], upper)
            out_ref[0, n, :half, cols] = (base_ref[0, n, :half, cols].astype(jnp.float32) + lower).astype(jnp.bfloat16)
            out_ref[0, n, half:, cols] = (base_ref[0, n, half:, cols].astype(jnp.float32) + upper).astype(jnp.bfloat16)


def whole(shape):
    return pl.BlockSpec(shape, lambda *steps: (0,) * len(shape))


def params(axes):
    return pltpu.CompilerParams(dimension_semantics=("arbitrary",) * axes, vmem_limit_bytes=VMEM_LIMIT)


def per_device(vertex, loop_matrix, own_mix, cross_mix, shells, partner, grid_index):
    places = lax.axis_size("mom") * lax.axis_size("bond")
    place = lax.axis_index("mom") * lax.axis_size("bond") + lax.axis_index("bond")
    channels, mom_local, bonds, _ = vertex.shape
    count = grid_index.shape[0]
    half = bonds // 2
    group = half // places
    tiles = bonds // LANES
    bf16 = jnp.bfloat16
    first = list(range(channels))
    send_groups = [first[:1], first[1:]]
    back_groups = [first[:-1], first[-1:]]

    lower_partner = partner[:half] - half
    uppers = jnp.arange(half, dtype=jnp.int32)
    pick = (lower_partner[:, None] == uppers[None, :]).astype(bf16)
    spread = pick.T

    wide = pltpu.VMEM((tiles, bonds * mom_local, LANES), jnp.float32)
    square = (half, half)
    matmul = 2 * mom_local * bonds**3
    field_bytes = 2 * mom_local * bonds * bonds
    field = jax.ShapeDtypeStruct(vertex.shape, bf16)
    token_shape = jax.ShapeDtypeStruct((8, LANES), jnp.float32)

    def flow(members):
        return jax.ShapeDtypeStruct((places, members, 2, group, mom_local, bonds), bf16)

    def one_flow():
        return pl.BlockSpec((places, 1, 2, group, mom_local, bonds), lambda c, i: (0, c, 0, 0, 0, 0))

    def matrix_at(start):
        return pl.BlockSpec((1, 1, bonds, bonds), lambda c, i: (c + start, i, 0, 0))

    def exchange(outgoing):
        return lax.all_to_all(outgoing, AXES, split_axis=0, concat_axis=0, tiled=True)

    pair = PAIR if mom_local % PAIR == 0 else 1
    plain = jax.ShapeDtypeStruct((places, 1, mom_local, 2, group, bonds), bf16)
    plain_block = pl.BlockSpec((places, 1, pair, 2, group, bonds), lambda i: (0, 0, i, 0, 0, 0))

    def pair_at(start):
        return pl.BlockSpec((1, pair, bonds, bonds), lambda i: (start, i, 0, 0))

    base, outgoing, token = pl.pallas_call(
        functools.partial(first_product_kernel, places),
        grid=(mom_local // pair,),
        in_specs=[pair_at(0), pair_at(0), whole(square), whole(square)],
        out_specs=[pair_at(0), plain_block, whole(token_shape.shape)],
        out_shape=[field, plain, token_shape],
        compiler_params=params(1),
        cost_estimate=pl.CostEstimate(flops=5 * matmul // 2, bytes_accessed=4 * field_bytes, transcendentals=0),
        name="product_first",
    )(vertex, loop_matrix, pick, spread)
    whole_rows = with_layout_constraint(exchange(outgoing), Layout(major_to_minor=tuple(range(6))))
    arrived = [whole_rows.transpose(0, 1, 3, 4, 2, 5)]
    for members in send_groups[1:]:
        matrix = matrix_at(members[0])
        size = len(members)
        base, outgoing, _ = pl.pallas_call(
            functools.partial(product_kernel, mom_local, places),
            grid=(size, mom_local),
            in_specs=[matrix, matrix, whole(square), whole(square)]
            + [pl.BlockSpec(memory_space=pl.ANY)],
            out_specs=[matrix, one_flow(), whole(token_shape.shape)],
            out_shape=[field, flow(size), token_shape],
            input_output_aliases={4: 0},
            scratch_shapes=[wide],
            compiler_params=params(2),
            cost_estimate=pl.CostEstimate(
                flops=5 * size * matmul // 2, bytes_accessed=4 * size * field_bytes, transcendentals=0
            ),
            name="product_%d" % members[0],
        )(vertex, loop_matrix, pick, spread, base)
        arrived.append(exchange(outgoing))

    shells, partner, grid_index, own_mix, cross_mix, _ = lax.optimization_barrier(
        (shells, partner, grid_index, own_mix, cross_mix, token)
    )
    plus_table = cas_table(grid_index, False)
    minus_table = cas_table(grid_index, True)
    back_table = plus_table.T
    cycle = cycle_index(count)[:, None]
    shell_order = jnp.concatenate([shells[:half], jnp.take(shells, partner[:half])])
    shell_rows = lax.dynamic_slice_in_dim(shell_order.reshape(2, half), place * group, group, axis=1)
    reach = (shell_rows[:, :, None] + shell_order[None, None, :]).reshape(2, group, 1, bonds)
    own_scaled = own_mix * (1.0 / count)
    cross_scaled = cross_mix * (1.0 / count)

    rows = ROWS if group % ROWS == 0 else 1

    def row_block(members):
        return pl.BlockSpec((places, members, 2, rows, mom_local, bonds), lambda i: (0, 0, 0, i, 0, 0))

    table = whole((count, count))
    scalars = pl.BlockSpec(memory_space=pltpu.SMEM)
    sizes = [len(members) for members in send_groups]
    finished, earlier = [], []
    for members in back_groups:
        size = len(members)
        outgoing = pl.pallas_call(
            functools.partial(lattice_kernel, sizes, members),
            grid=(group // rows,),
            in_specs=[
                scalars,
                scalars,
                table,
                table,
                table,
                whole((count, 1)),
                pl.BlockSpec((2, rows, 1, bonds), lambda i: (0, i, 0, 0)),
            ]
            + [row_block(n) for n in sizes]
            + [pl.BlockSpec(memory_space=pl.ANY)] * len(earlier),
            out_specs=row_block(size),
            out_shape=flow(size),
            compiler_params=params(1),
            cost_estimate=pl.CostEstimate(
                flops=(2 * channels + size) * 2 * count * count * 2 * group * bonds,
                bytes_accessed=(channels + size) * field_bytes,
                transcendentals=0,
            ),
            name="lattice_%d" % members[0],
        )(own_scaled, cross_scaled, plus_table, minus_table, back_table, cycle, reach, *arrived, *earlier)
        earlier = [outgoing]
        if members is back_groups[-1]:
            outgoing = outgoing.transpose(0, 1, 4, 2, 3, 5)
        finished.append(exchange(outgoing))

    for members, received in zip(back_groups[:-1], finished[:-1]):
        matrix = matrix_at(members[0])
        size = len(members)
        base = pl.pallas_call(
            functools.partial(finish_kernel, mom_local),
            grid=(size, mom_local),
            in_specs=[matrix, one_flow(), whole(square), whole(square)],
            out_specs=matrix,
            out_shape=field,
            input_output_aliases={0: 0},
            scratch_shapes=[wide],
            compiler_params=params(2),
            cost_estimate=pl.CostEstimate(
                flops=size * matmul // 2, bytes_accessed=3 * size * field_bytes, transcendentals=0
            ),
            name="finish_%d" % members[0],
        )(base, received, pick, spread)
    last = back_groups[-1][0]
    return pl.pallas_call(
        last_finish_kernel,
        grid=(mom_local // pair,),
        in_specs=[pair_at(last), plain_block, whole(square), whole(square)],
        out_specs=pair_at(last),
        out_shape=field,
        input_output_aliases={0: 0},
        compiler_params=params(1),
        cost_estimate=pl.CostEstimate(flops=matmul // 2, bytes_accessed=3 * field_bytes, transcendentals=0),
        name="finish_last",
    )(base, finished[-1], pick, spread)


def solution(mesh):
    in_specs = (P(None, AXES, None, None), P(None, AXES, None, None), P(), P(), P(), P(), P())
    return jax.shard_map(
        per_device, mesh=mesh, in_specs=in_specs, out_specs=P(None, AXES, None, None), check_vma=False
    )
```
